32 devices in a mesh: ctx: 16 (over z, y, core), fsdp: 2 (over x).
Axes of the slice: x: 2, y: 2, z: 4, core: 2. Of those that a mesh axis runs over, the one named last changes fastest.
Arguments:
- tokens: bfloat16 [2048, 8192], P('ctx', 'fsdp'), may hold values from -6 to 6
- kv_weight: bfloat16 [8192, 512], P('fsdp'), may hold values from -0.0625 to 0.0625
- queries: bfloat16 [2048, 1024], P('ctx', 'fsdp'), may hold values from -360 to 360
- relaxation: float32 [8], P('fsdp'), may hold values from 0.3 to 1
Outputs:
- attention: bfloat16 [2048, 1024], P('ctx', 'fsdp')
The draws below stay inside these ranges and needn't reach their ends.
All inputs are finite; a program needn't handle non-finite values.
Results may differ from the reference program's by a relative error of at most 0.0075.
The reference program's roundings to bfloat16 on the way (of `key_heads`, `value_heads` and `weights`) count: a program that leaves them out, or rounds other values in their place, can miss the bound.
Values may be sent and summed in bfloat16 or wider, within the bound.
A program may use at most 128 MiB of HBM per device.

```python
import math
import jax
import jax.numpy as jnp
from jax import lax

D = 8192
HD = 128
QH_DEV = 4
ITERS = 2
KVH = 2
QHEADS = 8
SEQ = 2048


def draw_queries(key, part):
    normal_key = jax.random.fold_in(jax.random.fold_in(key, 17), 0)
    standard = jnp.clip(jax.random.normal(normal_key, (SEQ, QHEADS * HD), jnp.float32), -6.0, 6.0)
    return standard.astype(jnp.bfloat16)


def shard_levels(stream_key, dims, pieces, least, top_value):
    factor_of, own = 1.0, jax.random.fold_in(stream_key, 6)
    for position, parts in pieces:
        steps = jnp.exp(jax.random.uniform(jax.random.fold_in(own, position), (parts,), jnp.float32, least / len(pieces), top_value / len(pieces)))
        factor_of = factor_of * jnp.repeat(steps, dims[position] // parts).reshape([-1 if axis == position else 1 for axis in range(len(dims))])
    return factor_of


def scatter_about(key, dims, spread, limit, shards=(), kind=jnp.bfloat16):
    factor_of = shard_levels(key, dims, shards, -0.22, 0.18) if shards else 1.0
    result = jax.random.normal(key, dims, jnp.float32) * spread * factor_of
    return jnp.minimum(jnp.maximum(result, -limit), limit).astype(kind)


def setup_inputs(seed: int = 0) -> dict:
    arg_keys = jax.random.split(jax.random.key(seed), 5)
    tokens = scatter_about(arg_keys[0], (SEQ, D), 1.0, 6.0, ((0, 16), (1, 2)))
    kv_weight = scatter_about(arg_keys[1], (D, 2 * HD * KVH), D ** -0.5, 0.0625, ((0, 2),))
    queries = draw_queries(jax.random.fold_in(arg_keys[4], 71), 0)
    relaxation = jnp.clip(jnp.exp(math.log(1.0) - 1.2039728 * jax.random.uniform(arg_keys[3], (QHEADS,), jnp.float32) ** shard_levels(arg_keys[3], (QHEADS,), ((0, 2),), -0.2, 0.2)), 0.3, 1.0)
    return dict(tokens=tokens, kv_weight=kv_weight, queries=queries, relaxation=relaxation)


ROPE_BASE = 500000.0

def rotate(key_rows, positions):
    half_width = key_rows.shape[-1] // 2
    frequency = jnp.exp(jnp.arange(half_width).astype(jnp.float32) * (-2.0 * math.log(ROPE_BASE) / key_rows.shape[-1]))
    angles = positions[:, None] * frequency[None, :]
    cosine = jnp.cos(angles)
    sine_part = jnp.sin(angles)
    front_half = key_rows[:, :half_width]
    back_half = key_rows[:, half_width:]
    return jnp.concatenate([front_half * cosine - back_half * sine_part, back_half * cosine + front_half * sine_part], axis=1)

def reference(tokens, kv_weight, queries, relaxation):
    length_all = tokens.shape[0]
    kv_full = jnp.dot(tokens, kv_weight, preferred_element_type=jnp.float32).reshape(length_all, KVH, 2, HD)
    positions = jnp.arange(length_all).astype(jnp.float32)
    key_heads = jax.vmap(rotate, in_axes=(1, None), out_axes=0)(kv_full[:, :, 0, :], positions).astype(jnp.bfloat16)
    value_heads = jnp.transpose(kv_full[:, :, 1, :], (1, 0, 2)).astype(jnp.bfloat16)
    query_heads = jnp.transpose(queries.reshape(length_all, QHEADS, HD), (1, 0, 2))
    kv_group = (jnp.arange(QHEADS) // QH_DEV).astype(jnp.int32)

    def one_head(member):
        query_rows, group_index, relax_rate = member
        key_rows = key_heads[group_index]
        value_rows = value_heads[group_index]
        scores = jnp.dot(query_rows, key_rows.T, preferred_element_type=jnp.float32) * (1.0 / math.sqrt(HD))
        column_pot = jnp.zeros((length_all,), jnp.float32)
        for iteration in range(ITERS):
            row_pot = -relax_rate * jax.nn.logsumexp(scores + column_pot[None, :], axis=1)
            column_pot = -relax_rate * jax.nn.logsumexp(scores + row_pot[:, None], axis=0)
        shifted = scores + column_pot[None, :]
        weights = jnp.exp(shifted - lax.optimization_barrier(jnp.max(shifted, axis=1, keepdims=True)))
        totals = lax.optimization_barrier(jnp.sum(weights, axis=1))
        blended = jnp.dot(weights.astype(jnp.bfloat16), value_rows, preferred_element_type=jnp.float32)
        return (blended / totals[:, None]).astype(jnp.bfloat16)
    head_outputs = lax.map(one_head, (query_heads, kv_group, relaxation))
    return jnp.transpose(head_outputs, (1, 0, 2)).reshape(length_all, QHEADS * HD)
```

```python
import functools
import math

import jax
import jax.numpy as jnp
from jax import lax
from jax.experimental import pallas as pl
from jax.experimental.pallas import tpu as pltpu
from jax.sharding import PartitionSpec as P

ITERS = 2
ROPE_BASE = 500000.0
LOG2E = 1.0 / math.log(2.0)
MESH = pl.DeviceIdType.MESH
CHUNKS = 4
ROWS = 64
LINE, ACROSS, CORE, CORNER = 0, 1, 2, 3


def xor(index, mask):
    bit = 1
    while bit <= mask:
        if mask & bit:
            index = index + bit - 2 * bit * ((index // bit) % 2)
        bit *= 2
    return index


def kernel(
    ctx_size, fsdp_size, quad,
    tok_hbm, w_hbm, q_hbm, rel_ref, out_ref,
    tok, w, q, keys, values, part_out, part_in, scores, rowp, colmax, colsum, colpot, lse, heads, landed,
    load_sem, q_local, q_send, q_recv, p_send, p_recv, b_send, b_recv, l_send, l_recv, o_send, o_recv,
):
    me = lax.axis_index("ctx")
    mf = lax.axis_index("fsdp")
    groups = ctx_size // quad
    z, m = me // quad, me % quad
    rows, depth = tok.shape
    hd = q.shape[-1]
    span = quad * rows
    step = depth // CHUNKS

    def at(index):
        return (index, mf)

    loads = {}
    for order, off in enumerate(list(range(1, fsdp_size)) + [0]):
        slot = pl.multiple_of(((mf + off) % fsdp_size) * 2 * hd, 2 * hd)
        for c in range(CHUNKS):
            piece = pl.ds(c * step, step)
            if order == 0:
                loads["t", c] = pltpu.make_async_copy(tok_hbm.at[:, piece], tok.at[:, piece], load_sem.at[fsdp_size, c])
                loads["t", c].start()
            loads[off, c] = pltpu.make_async_copy(
                w_hbm.at[piece, pl.ds(slot, 2 * hd)], w.at[off, piece], load_sem.at[off, c]
            )
            loads[off, c].start()

    barrier = pltpu.get_barrier_semaphore()
    peers = [(me, (mf + off) % fsdp_size) for off in range(1, fsdp_size)]
    peers += [at(xor(z, k) * quad + m) for k in range(1, groups)]
    peers += [at(z * quad + xor(m, k)) for k in range(1, quad)]
    for peer in peers:
        pl.semaphore_signal(barrier, inc=1, device_id=peer, device_id_type=MESH)

    lane = lax.broadcasted_iota(jnp.int32, (rows, hd), 1)
    position = (me * rows + lax.broadcasted_iota(jnp.int32, (rows, hd), 0)).astype(jnp.float32)
    turn = jnp.exp((lane % (hd // 2)).astype(jnp.float32) * (-2.0 * math.log(ROPE_BASE) / hd))
    angle = position * turn
    cosine = jnp.cos(angle)
    sine = jnp.sin(angle)
    sine = jnp.where(lane < hd // 2, -sine, sine)

    pl.semaphore_wait(barrier, len(peers))

    own_q = pltpu.make_async_copy(q_hbm.at[:, pl.ds(pl.multiple_of(m * hd, hd), hd)], q.at[0], q_local)
    own_q.start()
    q_copies = []
    for k in range(1, quad):
        peer = xor(m, k)
        q_copies.append(pltpu.make_async_remote_copy(
            src_ref=q_hbm.at[:, pl.ds(pl.multiple_of(peer * hd, hd), hd)], dst_ref=q.at[k],
            send_sem=q_send.at[k], recv_sem=q_recv.at[k], device_id=at(z * quad + peer), device_id_type=MESH,
        ))
        q_copies[-1].start()

    def project(off, first):
        total = jnp.zeros((rows, 2 * hd), jnp.float32)
        for c in range(CHUNKS):
            if first:
                loads["t", c].wait()
            loads[off, c].wait()
            piece = pl.ds(c * step, step)
            total = total + jnp.dot(tok[:, piece], w[off, piece], preferred_element_type=jnp.float32)
        return total

    p_copies = {}
    for off in range(1, fsdp_size):
        total = project(off, off == 1)
        for half in range(2):
            part_out[off - 1, half] = total[:, half * hd:(half + 1) * hd]
            p_copies[off, half] = pltpu.make_async_remote_copy(
                src_ref=part_out.at[off - 1, half], dst_ref=part_in.at[off - 1, half],
                send_sem=p_send.at[off - 1, half], recv_sem=p_recv.at[off - 1, half],
                device_id=(me, (mf + off) % fsdp_size), device_id_type=MESH,
            )
            p_copies[off, half].start()
    own = project(0, fsdp_size == 1)

    def summed(half):
        total = own[:, half * hd:(half + 1) * hd]
        for off in range(1, fsdp_size):
            p_copies[off, half].wait_recv()
            total = total + part_in[off - 1, half]
        return total

    sent = []

    def ship(buffer, which, way, k, block, target):
        copy = pltpu.make_async_remote_copy(
            src_ref=buffer.at[block], dst_ref=buffer.at[block],
            send_sem=b_send.at[which, way, k], recv_sem=b_recv.at[which, way, k],
            device_id=at(target), device_id_type=MESH,
        )
        copy.start()
        sent.append(copy)

    def arrive(buffer, which, way, k, member):
        block = xor(z, k) * quad + member
        pltpu.make_async_remote_copy(
            src_ref=buffer.at[block], dst_ref=buffer.at[block],
            send_sem=b_send.at[which, way, k], recv_sem=b_recv.at[which, way, k],
            device_id=at(block), device_id_type=MESH,
        ).wait_recv()
        return block

    core, across = z * quad + xor(m, 1), z * quad + xor(m, 2)

    def launch(buffer, which):
        for k in range(groups - 1, 0, -1):
            ship(buffer, which, LINE, k, me, xor(z, k) * quad + m)
        ship(buffer, which, ACROSS, 0, me, across)
        ship(buffer, which, CORE, 0, me, core)

    def from_line(buffer, which, k):
        block = arrive(buffer, which, LINE, k, m)
        ship(buffer, which, ACROSS, k, block, across)
        ship(buffer, which, CORE, k, block, core)

    def from_across(buffer, which, k):
        block = arrive(buffer, which, ACROSS, k, xor(m, 2))
        ship(buffer, which, CORNER, k, block, core)

    def complete(buffer, which, k):
        arrive(buffer, which, CORE, k, xor(m, 1))
        arrive(buffer, which, CORNER, k, xor(m, 3))

    key_part = summed(0)
    keys[me] = (key_part * cosine + pltpu.roll(key_part, hd // 2, 1) * sine).astype(jnp.bfloat16)
    launch(keys, 0)
    values[me] = summed(1).astype(jnp.bfloat16)
    own_q.wait()
    for copy in q_copies:
        copy.wait_recv()

    scale = LOG2E / math.sqrt(hd)

    def score_group(k):
        first = xor(z, k)
        block = keys[pl.ds(first * quad, quad)].reshape(span, hd)
        for part in range(quad):
            piece = lax.dot_general(q[part], block, (((1,), (1,)), ((), ())), preferred_element_type=jnp.float32)
            scores[pl.ds(part * rows, rows), pl.ds(pl.multiple_of(first * span, span), span)] = piece * scale

    for k in range(1, groups):
        from_line(keys, 0, k)
        from_across(keys, 0, k - 1)
    launch(values, 1)
    for k in range(groups - 1):
        complete(keys, 0, k)
        score_group(k)
    from_across(keys, 0, groups - 1)
    complete(keys, 0, groups - 1)
    score_group(groups - 1)

    rate = rel_ref[m]
    seq = scores.shape[1]
    blocks = span // ROWS

    def shifted(part, first):
        block = scores[part, :]
        if first:
            return block
        return (block.reshape(ROWS // 8, 8, seq) + colpot[...][None]).reshape(ROWS, seq)

    for it in range(ITERS):
        colmax[...] = jnp.full_like(colmax, -jnp.inf)

        @pl.loop(0, blocks)
        def _(i):
            part = pl.ds(pl.multiple_of(i * ROWS, ROWS), ROWS)
            peak = jnp.max(shifted(part, it == 0), axis=1, keepdims=True)
            mass = jnp.sum(jnp.exp2(shifted(part, it == 0) - peak), axis=1, keepdims=True)
            pot = -rate * (peak + jnp.log2(mass))
            rowp[part, :] = pot
            colmax[...] = jnp.maximum(colmax[...], jnp.max((scores[part, :] + pot).reshape(ROWS // 8, 8, seq), axis=0))

        top = jnp.max(colmax[...], axis=0, keepdims=True)
        colsum[...] = jnp.zeros_like(colsum)
        colmax[...] = jnp.broadcast_to(top, colmax.shape)

        @pl.loop(0, blocks)
        def _(i):
            part = pl.ds(pl.multiple_of(i * ROWS, ROWS), ROWS)
            lifted = (scores[part, :] + rowp[part, :]).reshape(ROWS // 8, 8, seq) - colmax[...][None]
            colsum[...] += jnp.sum(jnp.exp2(lifted), axis=0)

        lse[it, z] = top + jnp.log2(jnp.sum(colsum[...], axis=0, keepdims=True))
        for k in range(groups - 1, 0, -1):
            copy = pltpu.make_async_remote_copy(
                src_ref=lse.at[it, z], dst_ref=lse.at[it, z], send_sem=l_send.at[it, k], recv_sem=l_recv.at[it, k],
                device_id=at(xor(z, k) * quad + m), device_id_type=MESH,
            )
            copy.start()
            sent.append(copy)
        if it == 0:
            for k in range(1, groups):
                from_line(values, 1, k)
        if it == ITERS - 1:
            for k in range(groups):
                from_across(values, 1, k)
        for k in range(1, groups):
            other = xor(z, k)
            pltpu.make_async_remote_copy(
                src_ref=lse.at[it, other], dst_ref=lse.at[it, other], send_sem=l_send.at[it, k],
                recv_sem=l_recv.at[it, k], device_id=at(other * quad + m), device_id_type=MESH,
            ).wait_recv()
        terms = [lse[it, g] for g in range(groups)]
        top = functools.reduce(jnp.maximum, terms)
        mass = functools.reduce(jnp.add, [jnp.exp2(term - top) for term in terms])
        colpot[...] = jnp.broadcast_to(-rate * (top + jnp.log2(mass)), colpot.shape)

    for k in range(groups):
        complete(values, 1, k)
    value_rows = values[...].reshape(seq, hd)

    o_copies = []
    for k in range(quad - 1, -1, -1):
        numer = []
        for half in range(rows // ROWS):
            part = pl.ds(k * rows + half * ROWS, ROWS)
            peak = jnp.max(shifted(part, False), axis=1, keepdims=True)
            weights = jnp.exp2(shifted(part, False) - peak)
            total = jnp.sum(weights, axis=1, keepdims=True)
            blended = jnp.dot(weights.astype(jnp.bfloat16), value_rows, preferred_element_type=jnp.float32)
            heads[k, pl.ds(half * ROWS, ROWS), :] = (blended / total).astype(jnp.bfloat16)
        if k:
            o_copies.append(pltpu.make_async_remote_copy(
                src_ref=heads.at[k], dst_ref=landed.at[k], send_sem=o_send.at[k], recv_sem=o_recv.at[k],
                device_id=at(z * quad + xor(m, k)), device_id_type=MESH,
            ))
            o_copies[-1].start()
    out_ref[:, pl.ds(pl.multiple_of(m * hd, hd), hd)] = heads[0]
    for k, copy in zip(range(quad - 1, 0, -1), o_copies):
        copy.wait_recv()
        out_ref[:, pl.ds(pl.multiple_of(xor(m, k) * hd, hd), hd)] = landed[k]
    for copy in q_copies + list(p_copies.values()) + sent + o_copies:
        copy.wait_send()


def on_device(ctx_size, fsdp_size, tokens, kv_weight, queries, relaxation):
    rows, depth = tokens.shape
    quad = relaxation.shape[0]
    groups = ctx_size // quad
    hd = kv_weight.shape[1] // fsdp_size // 2
    seq = ctx_size * rows
    bf16, f32 = jnp.bfloat16, jnp.float32
    dma = pltpu.SemaphoreType.DMA
    others = max(fsdp_size - 1, 1)
    return pl.pallas_call(
        functools.partial(kernel, ctx_size, fsdp_size, quad),
        out_shape=jax.ShapeDtypeStruct(queries.shape, bf16),
        in_specs=[pl.BlockSpec(memory_space=pl.ANY)] * 3 + [pl.BlockSpec(memory_space=pltpu.SMEM)],
        out_specs=pl.BlockSpec(memory_space=pltpu.VMEM),
        scratch_shapes=[
            pltpu.VMEM((rows, depth), bf16),
            pltpu.VMEM((fsdp_size, depth, 2 * hd), bf16),
            pltpu.VMEM((quad, rows, hd), bf16),
            pltpu.VMEM((ctx_size, rows, hd), bf16),
            pltpu.VMEM((ctx_size, rows, hd), bf16),
            pltpu.VMEM((others, 2, rows, hd), f32),
            pltpu.VMEM((others, 2, rows, hd), f32),
            pltpu.VMEM((quad * rows, seq), f32),
            pltpu.VMEM((quad * rows, 1), f32),
            pltpu.VMEM((8, seq), f32),
            pltpu.VMEM((8, seq), f32),
            pltpu.VMEM((8, seq), f32),
            pltpu.VMEM((ITERS, groups, 1, seq), f32),
            pltpu.VMEM((quad, rows, hd), bf16),
            pltpu.VMEM((quad, rows, hd), bf16),
            dma((fsdp_size + 1, CHUNKS)),
            dma,
            dma((quad,)), dma((quad,)),
            dma((others, 2)), dma((others, 2)),
            dma((2, 4, groups)), dma((2, 4, groups)),
            dma((ITERS, groups)), dma((ITERS, groups)),
            dma((quad,)), dma((quad,)),
        ],
        compiler_params=pltpu.CompilerParams(
            collective_id=0, has_side_effects=True, vmem_limit_bytes=60 * 1024 * 1024
        ),
    )(tokens, kv_weight, queries, relaxation)


def solution(mesh):
    placed = (P("ctx", "fsdp"), P("fsdp", None), P("ctx", "fsdp"), P("fsdp"))
    body = functools.partial(on_device, mesh.shape["ctx"], mesh.shape["fsdp"])
    return jax.shard_map(body, mesh=mesh, in_specs=placed, out_specs=P("ctx", "fsdp"), check_vma=False)
```

```python
import functools
import math

import jax
import jax.numpy as jnp
from jax import lax
from jax.experimental import pallas as pl
from jax.experimental.pallas import tpu as pltpu
from jax.sharding import PartitionSpec as P

ITERS = 2
ROPE_BASE = 500000.0
LOG2E = 1.0 / math.log(2.0)
MESH = pl.DeviceIdType.MESH
CHUNKS = 4
ROWS = 128
OUT_ROWS = 64
LINE, ACROSS, CORE, CORNER = 0, 1, 2, 3


def xor(index, mask):
    bit = 1
    while bit <= mask:
        if mask & bit:
            index = index + bit - 2 * bit * ((index // bit) % 2)
        bit *= 2
    return index


def kernel(
    ctx_size, fsdp_size, quad,
    tok_hbm, w_hbm, q_hbm, rel_ref, out_ref,
    tok, w, q, keys, values, part_out, part_in, scores, rowp, colmax, colsum, colpot, lse, heads, landed,
    load_sem, q_local, q_send, q_recv, p_send, p_recv, b_send, b_recv, l_send, l_recv, o_send, o_recv,
):
    me = lax.axis_index("ctx")
    mf = lax.axis_index("fsdp")
    groups = ctx_size // quad
    z, m = me // quad, me % quad
    rows, depth = tok.shape
    hd = q.shape[-1]
    span = quad * rows
    step = depth // CHUNKS

    def at(index):
        return (index, mf)

    loads = {}
    for order, off in enumerate(list(range(1, fsdp_size)) + [0]):
        slot = pl.multiple_of(((mf + off) % fsdp_size) * 2 * hd, 2 * hd)
        for c in range(CHUNKS):
            piece = pl.ds(c * step, step)
            if order == 0:
                loads["t", c] = pltpu.make_async_copy(tok_hbm.at[:, piece], tok.at[:, piece], load_sem.at[fsdp_size, c])
                loads["t", c].start()
            loads[off, c] = pltpu.make_async_copy(
                w_hbm.at[piece, pl.ds(slot, 2 * hd)], w.at[off, piece], load_sem.at[off, c]
            )
            loads[off, c].start()

    barrier = pltpu.get_barrier_semaphore()
    peers = [(me, (mf + off) % fsdp_size) for off in range(1, fsdp_size)]
    peers += [at(xor(z, k) * quad + m) for k in range(1, groups)]
    peers += [at(z * quad + xor(m, k)) for k in range(1, quad)]
    for peer in peers:
        pl.semaphore_signal(barrier, inc=1, device_id=peer, device_id_type=MESH)

    lane = lax.broadcasted_iota(jnp.int32, (rows, hd), 1)
    position = (me * rows + lax.broadcasted_iota(jnp.int32, (rows, hd), 0)).astype(jnp.float32)
    turn = jnp.exp((lane % (hd // 2)).astype(jnp.float32) * (-2.0 * math.log(ROPE_BASE) / hd))
    angle = position * turn
    cosine = jnp.cos(angle)
    sine = jnp.sin(angle)
    sine = jnp.where(lane < hd // 2, -sine, sine)

    def project(off, first):
        total = jnp.zeros((rows, 2 * hd), jnp.float32)
        for c in range(CHUNKS):
            if first:
                loads["t", c].wait()
            loads[off, c].wait()
            piece = pl.ds(c * step, step)
            total = total + jnp.dot(tok[:, piece], w[off, piece], preferred_element_type=jnp.float32)
        return total

    totals = [project(off, off == 1) for off in range(1, fsdp_size)]
    own = project(0, fsdp_size == 1)
    for off in range(1, fsdp_size):
        for half in range(2):
            part_out[off - 1, half] = totals[off - 1][:, half * hd:(half + 1) * hd]

    pl.semaphore_wait(barrier, len(peers))

    p_copies = {}
    for half in range(2):
        for off in range(1, fsdp_size):
            p_copies[off, half] = pltpu.make_async_remote_copy(
                src_ref=part_out.at[off - 1, half], dst_ref=part_in.at[off - 1, half],
                send_sem=p_send.at[off - 1, half], recv_sem=p_recv.at[off - 1, half],
                device_id=(me, (mf + off) % fsdp_size), device_id_type=MESH,
            )
            p_copies[off, half].start()

    own_q = pltpu.make_async_copy(q_hbm.at[:, pl.ds(pl.multiple_of(m * hd, hd), hd)], q.at[0], q_local)
    own_q.start()
    q_copies = []
    for k in range(1, quad):
        peer = xor(m, k)
        q_copies.append(pltpu.make_async_remote_copy(
            src_ref=q_hbm.at[:, pl.ds(pl.multiple_of(peer * hd, hd), hd)], dst_ref=q.at[k],
            send_sem=q_send.at[k], recv_sem=q_recv.at[k], device_id=at(z * quad + peer), device_id_type=MESH,
        ))
        q_copies[-1].start()

    def summed(half):
        total = own[:, half * hd:(half + 1) * hd]
        for off in range(1, fsdp_size):
            p_copies[off, half].wait_recv()
            total = total + part_in[off - 1, half]
        return total

    sent = []

    def ship(buffer, which, way, k, block, target):
        copy = pltpu.make_async_remote_copy(
            src_ref=buffer.at[block], dst_ref=buffer.at[block],
            send_sem=b_send.at[which, way, k], recv_sem=b_recv.at[which, way, k],
            device_id=at(target), device_id_type=MESH,
        )
        copy.start()
        sent.append(copy)

    def arrive(buffer, which, way, k, member):
        block = xor(z, k) * quad + member
        pltpu.make_async_remote_copy(
            src_ref=buffer.at[block], dst_ref=buffer.at[block],
            send_sem=b_send.at[which, way, k], recv_sem=b_recv.at[which, way, k],
            device_id=at(block), device_id_type=MESH,
        ).wait_recv()
        return block

    core, across = z * quad + xor(m, 1), z * quad + xor(m, 2)

    def launch(buffer, which):
        for k in range(groups - 1, 0, -1):
            ship(buffer, which, LINE, k, me, xor(z, k) * quad + m)
        ship(buffer, which, ACROSS, 0, me, across)
        ship(buffer, which, CORE, 0, me, core)

    def from_line(buffer, which, k):
        block = arrive(buffer, which, LINE, k, m)
        ship(buffer, which, ACROSS, k, block, across)
        ship(buffer, which, CORE, k, block, core)

    def from_across(buffer, which, k):
        block = arrive(buffer, which, ACROSS, k, xor(m, 2))
        ship(buffer, which, CORNER, k, block, core)

    def complete(buffer, which, k):
        arrive(buffer, which, CORE, k, xor(m, 1))
        arrive(buffer, which, CORNER, k, xor(m, 3))

    key_part = summed(0)
    keys[me] = (key_part * cosine + pltpu.roll(key_part, hd // 2, 1) * sine).astype(jnp.bfloat16)
    launch(keys, 0)
    values[me] = summed(1).astype(jnp.bfloat16)
    own_q.wait()
    for copy in q_copies:
        copy.wait_recv()

    scale = LOG2E / math.sqrt(hd)

    def score_group(k):
        first = xor(z, k)
        block = keys[pl.ds(first * quad, quad)].reshape(span, hd)
        for part in range(quad):
            piece = lax.dot_general(q[part], block, (((1,), (1,)), ((), ())), preferred_element_type=jnp.float32)
            scores[pl.ds(part * rows, rows), pl.ds(pl.multiple_of(first * span, span), span)] = piece * scale

    for k in range(1, groups):
        from_line(keys, 0, k)
        from_across(keys, 0, k - 1)
    launch(values, 1)
    for k in range(groups - 1):
        complete(keys, 0, k)
        score_group(k)
    from_across(keys, 0, groups - 1)
    complete(keys, 0, groups - 1)
    score_group(groups - 1)

    rate = rel_ref[m]
    seq = scores.shape[1]
    blocks = span // ROWS

    def shifted(part, first):
        block = scores[part, :]
        if first:
            return block
        return (block.reshape(-1, 8, seq) + colpot[...][None]).reshape(block.shape)

    for it in range(ITERS):
        colmax[...] = jnp.full_like(colmax, -jnp.inf)

        @pl.loop(0, blocks)
        def _(i):
            part = pl.ds(pl.multiple_of(i * ROWS, ROWS), ROWS)
            peak = jnp.max(shifted(part, it == 0), axis=1, keepdims=True)
            mass = jnp.sum(jnp.exp2(shifted(part, it == 0) - peak), axis=1, keepdims=True)
            pot = -rate * (peak + jnp.log2(mass))
            rowp[part, :] = pot
            colmax[...] = jnp.maximum(colmax[...], jnp.max((scores[part, :] + pot).reshape(ROWS // 8, 8, seq), axis=0))

        top = jnp.max(colmax[...], axis=0, keepdims=True)
        colsum[...] = jnp.zeros_like(colsum)
        colmax[...] = jnp.broadcast_to(top, colmax.shape)

        @pl.loop(0, blocks)
        def _(i):
            part = pl.ds(pl.multiple_of(i * ROWS, ROWS), ROWS)
            lifted = (scores[part, :] + rowp[part, :]).reshape(ROWS // 8, 8, seq) - colmax[...][None]
            colsum[...] += jnp.sum(jnp.exp2(lifted), axis=0)

        lse[it, z] = top + jnp.log2(jnp.sum(colsum[...], axis=0, keepdims=True))
        for k in range(groups - 1, 0, -1):
            copy = pltpu.make_async_remote_copy(
                src_ref=lse.at[it, z], dst_ref=lse.at[it, z], send_sem=l_send.at[it, k], recv_sem=l_recv.at[it, k],
                device_id=at(xor(z, k) * quad + m), device_id_type=MESH,
            )
            copy.start()
            sent.append(copy)
        if it == 0:
            for k in range(1, groups):
                from_line(values, 1, k)
        if it == ITERS - 1:
            for k in range(groups):
                from_across(values, 1, k)
        for k in range(1, groups):
            other = xor(z, k)
            pltpu.make_async_remote_copy(
                src_ref=lse.at[it, other], dst_ref=lse.at[it, other], send_sem=l_send.at[it, k],
                recv_sem=l_recv.at[it, k], device_id=at(other * quad + m), device_id_type=MESH,
            ).wait_recv()
        terms = [lse[it, g] for g in range(groups)]
        top = functools.reduce(jnp.maximum, terms)
        mass = functools.reduce(jnp.add, [jnp.exp2(term - top) for term in terms])
        colpot[...] = jnp.broadcast_to(-rate * (top + jnp.log2(mass)), colpot.shape)

    for k in range(groups):
        complete(values, 1, k)
    value_rows = values[...].reshape(seq, hd)

    o_copies = []
    for k in range(quad - 1, -1, -1):
        for half in range(rows // OUT_ROWS):
            part = pl.ds(k * rows + half * OUT_ROWS, OUT_ROWS)
            peak = jnp.max(shifted(part, False), axis=1, keepdims=True)
            weights = jnp.exp2(shifted(part, False) - peak)
            total = jnp.sum(weights, axis=1, keepdims=True)
            blended = jnp.dot(weights.astype(jnp.bfloat16), value_rows, preferred_element_type=jnp.float32)
            heads[k, pl.ds(half * OUT_ROWS, OUT_ROWS), :] = (blended / total).astype(jnp.bfloat16)
        if k:
            o_copies.append(pltpu.make_async_remote_copy(
                src_ref=heads.at[k], dst_ref=landed.at[k], send_sem=o_send.at[k], recv_sem=o_recv.at[k],
                device_id=at(z * quad + xor(m, k)), device_id_type=MESH,
            ))
            o_copies[-1].start()
    out_ref[:, pl.ds(pl.multiple_of(m * hd, hd), hd)] = heads[0]
    for k, copy in zip(range(quad - 1, 0, -1), o_copies):
        copy.wait_recv()
        out_ref[:, pl.ds(pl.multiple_of(xor(m, k) * hd, hd), hd)] = landed[k]
    for copy in q_copies + list(p_copies.values()) + sent + o_copies:
        copy.wait_send()


def on_device(ctx_size, fsdp_size, tokens, kv_weight, queries, relaxation):
    rows, depth = tokens.shape
    quad = relaxation.shape[0]
    groups = ctx_size // quad
    hd = kv_weight.shape[1] // fsdp_size // 2
    seq = ctx_size * rows
    bf16, f32 = jnp.bfloat16, jnp.float32
    dma = pltpu.SemaphoreType.DMA
    others = max(fsdp_size - 1, 1)
    in_hbm = [pltpu.with_memory_space_constraint(a, pltpu.HBM) for a in (tokens, kv_weight, queries, relaxation)]
    return pl.pallas_call(
        functools.partial(kernel, ctx_size, fsdp_size, quad),
        out_shape=jax.ShapeDtypeStruct(queries.shape, bf16),
        in_specs=[pl.BlockSpec(memory_space=pl.ANY)] * 3 + [pl.BlockSpec(memory_space=pltpu.SMEM)],
        out_specs=pl.BlockSpec(memory_space=pltpu.VMEM),
        scratch_shapes=[
            pltpu.VMEM((rows, depth), bf16),
            pltpu.VMEM((fsdp_size, depth, 2 * hd), bf16),
            pltpu.VMEM((quad, rows, hd), bf16),
            pltpu.VMEM((ctx_size, rows, hd), bf16),
            pltpu.VMEM((ctx_size, rows, hd), bf16),
            pltpu.VMEM((others, 2, rows, hd), f32),
            pltpu.VMEM((others, 2, rows, hd), f32),
            pltpu.VMEM((quad * rows, seq), f32),
            pltpu.VMEM((quad * rows, 1), f32),
            pltpu.VMEM((8, seq), f32),
            pltpu.VMEM((8, seq), f32),
            pltpu.VMEM((8, seq), f32),
            pltpu.VMEM((ITERS, groups, 1, seq), f32),
            pltpu.VMEM((quad, rows, hd), bf16),
            pltpu.VMEM((quad, rows, hd), bf16),
            dma((fsdp_size + 1, CHUNKS)),
            dma,
            dma((quad,)), dma((quad,)),
            dma((others, 2)), dma((others, 2)),
            dma((2, 4, groups)), dma((2, 4, groups)),
            dma((ITERS, groups)), dma((ITERS, groups)),
            dma((quad,)), dma((quad,)),
        ],
        compiler_params=pltpu.CompilerParams(
            collective_id=0, has_side_effects=True, vmem_limit_bytes=52 * 1024 * 1024
        ),
    )(*in_hbm)


def solution(mesh):
    placed = (P("ctx", "fsdp"), P("fsdp", None), P("ctx", "fsdp"), P("fsdp"))
    body = functools.partial(on_device, mesh.shape["ctx"], mesh.shape["fsdp"])
    return jax.shard_map(body, mesh=mesh, in_specs=placed, out_specs=P("ctx", "fsdp"), check_vma=False)
```

```python
import functools
import math

import jax
import jax.numpy as jnp
from jax import lax
from jax.experimental import pallas as pl
from jax.experimental.pallas import tpu as pltpu
from jax.sharding import PartitionSpec as P

ITERS = 2
ROPE_BASE = 500000.0
LOG2E = 1.0 / math.log(2.0)
MESH = pl.DeviceIdType.MESH
CHUNKS = 4
ROWS = 256
OUT_ROWS = 64
LINE, ACROSS, CORE, CORNER = 0, 1, 2, 3


DIRECT = (2, 3)


def xor(index, mask):
    bit = 1
    while bit <= mask:
        if mask & bit:
            index = index + bit - 2 * bit * ((index // bit) % 2)
        bit *= 2
    return index


def kernel(
    ctx_size, fsdp_size, quad,
    tok_hbm, w_hbm, q_hbm, rel_ref, out_ref,
    tok, w, q, keys, values, part_out, part_in, scores, peaks, rowp, colmax, colsum, colpot, lse, heads, landed,
    load_sem, q_local, q_send, q_recv, p_send, p_recv, b_send, b_recv, l_send, l_recv, o_send, o_recv,
):
    me = lax.axis_index("ctx")
    mf = lax.axis_index("fsdp")
    groups = ctx_size // quad
    z, m = me // quad, me % quad
    rows, depth = tok.shape
    hd = q.shape[-1]
    span = quad * rows
    step = depth // CHUNKS

    def at(index):
        return (index, mf)

    loads = {}
    for order, off in enumerate(list(range(1, fsdp_size)) + [0]):
        slot = pl.multiple_of(((mf + off) % fsdp_size) * 2 * hd, 2 * hd)
        for c in range(CHUNKS):
            piece = pl.ds(c * step, step)
            if order == 0:
                loads["t", c] = pltpu.make_async_copy(tok_hbm.at[:, piece], tok.at[:, piece], load_sem.at[fsdp_size, c])
                loads["t", c].start()
            loads[off, c] = pltpu.make_async_copy(
                w_hbm.at[piece, pl.ds(slot, 2 * hd)], w.at[off, piece], load_sem.at[off, c]
            )
            loads[off, c].start()

    barrier = pltpu.get_barrier_semaphore()
    peers = [(me, (mf + off) % fsdp_size) for off in range(1, fsdp_size)]
    peers += [at(xor(z, k) * quad + m) for k in range(1, groups)]
    peers += [at(z * quad + xor(m, k)) for k in range(1, quad)]
    direct = [k for k in DIRECT if k < groups]
    peers += [at(xor(z, k) * quad + xor(m, 2)) for k in direct]
    for peer in peers:
        pl.semaphore_signal(barrier, inc=1, device_id=peer, device_id_type=MESH)

    lane = lax.broadcasted_iota(jnp.int32, (rows, hd), 1)
    position = (me * rows + lax.broadcasted_iota(jnp.int32, (rows, hd), 0)).astype(jnp.float32)
    turn = jnp.exp((lane % (hd // 2)).astype(jnp.float32) * (-2.0 * math.log(ROPE_BASE) / hd))
    angle = position * turn
    cosine = jnp.cos(angle)
    sine = jnp.sin(angle)
    sine = jnp.where(lane < hd // 2, -sine, sine)

    def project(off, first):
        total = jnp.zeros((rows, 2 * hd), jnp.float32)
        for c in range(CHUNKS):
            if first:
                loads["t", c].wait()
            loads[off, c].wait()
            piece = pl.ds(c * step, step)
            total = total + jnp.dot(tok[:, piece], w[off, piece], preferred_element_type=jnp.float32)
        return total

    totals = [project(off, off == 1) for off in range(1, fsdp_size)]
    own = project(0, fsdp_size == 1)
    for off in range(1, fsdp_size):
        for half in range(2):
            part_out[off - 1, half] = totals[off - 1][:, half * hd:(half + 1) * hd]

    pl.semaphore_wait(barrier, len(peers))

    p_copies = {}
    for half in range(2):
        for off in range(1, fsdp_size):
            p_copies[off, half] = pltpu.make_async_remote_copy(
                src_ref=part_out.at[off - 1, half], dst_ref=part_in.at[off - 1, half],
                send_sem=p_send.at[off - 1, half], recv_sem=p_recv.at[off - 1, half],
                device_id=(me, (mf + off) % fsdp_size), device_id_type=MESH,
            )
            p_copies[off, half].start()

    own_q = pltpu.make_async_copy(q_hbm.at[:, pl.ds(pl.multiple_of(m * hd, hd), hd)], q.at[0], q_local)
    own_q.start()
    q_copies = []
    for k in range(1, quad):
        peer = xor(m, k)
        q_copies.append(pltpu.make_async_remote_copy(
            src_ref=q_hbm.at[:, pl.ds(pl.multiple_of(peer * hd, hd), hd)], dst_ref=q.at[k],
            send_sem=q_send.at[k], recv_sem=q_recv.at[k], device_id=at(z * quad + peer), device_id_type=MESH,
        ))
        q_copies[-1].start()

    def summed(half):
        total = own[:, half * hd:(half + 1) * hd]
        for off in range(1, fsdp_size):
            p_copies[off, half].wait_recv()
            total = total + part_in[off - 1, half]
        return total

    sent = []

    def ship(buffer, which, way, k, block, target):
        copy = pltpu.make_async_remote_copy(
            src_ref=buffer.at[block], dst_ref=buffer.at[block],
            send_sem=b_send.at[which, way, k], recv_sem=b_recv.at[which, way, k],
            device_id=at(target), device_id_type=MESH,
        )
        copy.start()
        sent.append(copy)

    def arrive(buffer, which, way, k, member):
        block = xor(z, k) * quad + member
        pltpu.make_async_remote_copy(
            src_ref=buffer.at[block], dst_ref=buffer.at[block],
            send_sem=b_send.at[which, way, k], recv_sem=b_recv.at[which, way, k],
            device_id=at(block), device_id_type=MESH,
        ).wait_recv()
        return block

    core, across = z * quad + xor(m, 1), z * quad + xor(m, 2)

    def launch(buffer, which):
        for k in range(groups - 1, 0, -1):
            ship(buffer, which, LINE, k, me, xor(z, k) * quad + m)
        if which == 0:
            for k in direct:
                ship(buffer, which, ACROSS, k, me, xor(z, k) * quad + xor(m, 2))
        ship(buffer, which, ACROSS, 0, me, across)
        ship(buffer, which, CORE, 0, me, core)

    def from_line(buffer, which, k):
        block = arrive(buffer, which, LINE, k, m)
        if which == 1 or k not in direct:
            ship(buffer, which, ACROSS, k, block, across)
        ship(buffer, which, CORE, k, block, core)

    def from_across(buffer, which, k):
        block = arrive(buffer, which, ACROSS, k, xor(m, 2))
        ship(buffer, which, CORNER, k, block, core)

    def complete(buffer, which, k):
        arrive(buffer, which, CORE, k, xor(m, 1))
        arrive(buffer, which, CORNER, k, xor(m, 3))

    key_part = summed(0)
    keys[me] = (key_part * cosine + pltpu.roll(key_part, hd // 2, 1) * sine).astype(jnp.bfloat16)
    launch(keys, 0)
    values[me] = summed(1).astype(jnp.bfloat16)
    own_q.wait()
    for copy in q_copies:
        copy.wait_recv()

    scale = LOG2E / math.sqrt(hd)

    def score_group(k):
        first = xor(z, k)
        block = keys[pl.ds(first * quad, quad)].reshape(span, hd)
        for part in range(quad):
            piece = scale * lax.dot_general(
                q[part], block, (((1,), (1,)), ((), ())), preferred_element_type=jnp.float32
            )
            place = pl.ds(part * rows, rows)
            scores[place, pl.ds(pl.multiple_of(first * span, span), span)] = piece
            peak = jnp.max(piece, axis=1, keepdims=True)
            peaks[place, :] = jnp.maximum(peaks[place, :], peak) if k else peak

    for k in range(1, groups):
        from_line(keys, 0, k)
        from_across(keys, 0, k - 1)
    launch(values, 1)
    for k in range(groups):
        if k == max(groups - 2, 0):
            from_across(keys, 0, groups - 1)
        complete(keys, 0, k)
        score_group(k)

    rate = rel_ref[m]
    seq = scores.shape[1]
    blocks = span // ROWS

    def shifted(part, first):
        block = scores[part, :]
        if first:
            return block
        return (block.reshape(-1, 8, seq) + colpot[...][None]).reshape(block.shape)

    for it in range(ITERS):
        colmax[...] = jnp.full_like(colmax, -jnp.inf)

        @pl.loop(0, blocks)
        def _(i):
            part = pl.ds(pl.multiple_of(i * ROWS, ROWS), ROWS)
            peak = jnp.max(shifted(part, False), axis=1, keepdims=True) if it else peaks[part, :]
            mass = jnp.sum(jnp.exp2(shifted(part, it == 0) - peak), axis=1, keepdims=True)
            pot = -rate * (peak + jnp.log2(mass))
            rowp[part, :] = pot
            colmax[...] = jnp.maximum(colmax[...], jnp.max((scores[part, :] + pot).reshape(ROWS // 8, 8, seq), axis=0))

        top = jnp.max(colmax[...], axis=0, keepdims=True)
        colsum[...] = jnp.zeros_like(colsum)
        colmax[...] = jnp.broadcast_to(top, colmax.shape)

        @pl.loop(0, blocks)
        def _(i):
            part = pl.ds(pl.multiple_of(i * ROWS, ROWS), ROWS)
            lifted = (scores[part, :] + rowp[part, :]).reshape(ROWS // 8, 8, seq) - colmax[...][None]
            colsum[...] += jnp.sum(jnp.exp2(lifted), axis=0)

        lse[it, z] = top + jnp.log2(jnp.sum(colsum[...], axis=0, keepdims=True))
        for k in range(groups - 1, 0, -1):
            copy = pltpu.make_async_remote_copy(
                src_ref=lse.at[it, z], dst_ref=lse.at[it, z], send_sem=l_send.at[it, k], recv_sem=l_recv.at[it, k],
                device_id=at(xor(z, k) * quad + m), device_id_type=MESH,
            )
            copy.start()
            sent.append(copy)
        if it == 0:
            for k in range(1, groups):
                from_line(values, 1, k)
        if it == ITERS - 1:
            for k in range(groups):
                from_across(values, 1, k)
        for k in range(1, groups):
            other = xor(z, k)
            pltpu.make_async_remote_copy(
                src_ref=lse.at[it, other], dst_ref=lse.at[it, other], send_sem=l_send.at[it, k],
                recv_sem=l_recv.at[it, k], device_id=at(other * quad + m), device_id_type=MESH,
            ).wait_recv()
        terms = [lse[it, g] for g in range(groups)]
        top = functools.reduce(jnp.maximum, terms)
        mass = functools.reduce(jnp.add, [jnp.exp2(term - top) for term in terms])
        colpot[...] = jnp.broadcast_to(-rate * (top + jnp.log2(mass)), colpot.shape)

    for k in range(groups):
        complete(values, 1, k)
    value_rows = values[...].reshape(seq, hd)

    o_copies = []
    for k in range(quad - 1, -1, -1):
        for half in range(rows // OUT_ROWS):
            part = pl.ds(k * rows + half * OUT_ROWS, OUT_ROWS)
            peak = jnp.max(shifted(part, False), axis=1, keepdims=True)
            weights = jnp.exp2(shifted(part, False) - peak)
            total = jnp.sum(weights, axis=1, keepdims=True)
            blended = jnp.dot(weights.astype(jnp.bfloat16), value_rows, preferred_element_type=jnp.float32)
            heads[k, pl.ds(half * OUT_ROWS, OUT_ROWS), :] = (blended / total).astype(jnp.bfloat16)
        if k:
            o_copies.append(pltpu.make_async_remote_copy(
                src_ref=heads.at[k], dst_ref=landed.at[k], send_sem=o_send.at[k], recv_sem=o_recv.at[k],
                device_id=at(z * quad + xor(m, k)), device_id_type=MESH,
            ))
            o_copies[-1].start()
    out_ref[:, pl.ds(pl.multiple_of(m * hd, hd), hd)] = heads[0]
    for k, copy in zip(range(quad - 1, 0, -1), o_copies):
        copy.wait_recv()
        out_ref[:, pl.ds(pl.multiple_of(xor(m, k) * hd, hd), hd)] = landed[k]
    for copy in q_copies + list(p_copies.values()) + sent + o_copies:
        copy.wait_send()


def on_device(ctx_size, fsdp_size, tokens, kv_weight, queries, relaxation):
    rows, depth = tokens.shape
    quad = relaxation.shape[0]
    groups = ctx_size // quad
    hd = kv_weight.shape[1] // fsdp_size // 2
    seq = ctx_size * rows
    bf16, f32 = jnp.bfloat16, jnp.float32
    dma = pltpu.SemaphoreType.DMA
    others = max(fsdp_size - 1, 1)
    in_hbm = [pltpu.with_memory_space_constraint(a, pltpu.HBM) for a in (tokens, kv_weight, queries, relaxation)]
    return pl.pallas_call(
        functools.partial(kernel, ctx_size, fsdp_size, quad),
        out_shape=jax.ShapeDtypeStruct(queries.shape, bf16),
        in_specs=[pl.BlockSpec(memory_space=pl.ANY)] * 3 + [pl.BlockSpec(memory_space=pltpu.SMEM)],
        out_specs=pl.BlockSpec(memory_space=pltpu.VMEM),
        scratch_shapes=[
            pltpu.VMEM((rows, depth), bf16),
            pltpu.VMEM((fsdp_size, depth, 2 * hd), bf16),
            pltpu.VMEM((quad, rows, hd), bf16),
            pltpu.VMEM((ctx_size, rows, hd), bf16),
            pltpu.VMEM((ctx_size, rows, hd), bf16),
            pltpu.VMEM((others, 2, rows, hd), f32),
            pltpu.VMEM((others, 2, rows, hd), f32),
            pltpu.VMEM((quad * rows, seq), f32),
            pltpu.VMEM((quad * rows, 1), f32),
            pltpu.VMEM((quad * rows, 1), f32),
            pltpu.VMEM((8, seq), f32),
            pltpu.VMEM((8, seq), f32),
            pltpu.VMEM((8, seq), f32),
            pltpu.VMEM((ITERS, groups, 1, seq), f32),
            pltpu.VMEM((quad, rows, hd), bf16),
            pltpu.VMEM((quad, rows, hd), bf16),
            dma((fsdp_size + 1, CHUNKS)),
            dma,
            dma((quad,)), dma((quad,)),
            dma((others, 2)), dma((others, 2)),
            dma((2, 4, groups)), dma((2, 4, groups)),
            dma((ITERS, groups)), dma((ITERS, groups)),
            dma((quad,)), dma((quad,)),
        ],
        compiler_params=pltpu.CompilerParams(
            collective_id=0, has_side_effects=True, vmem_limit_bytes=52 * 1024 * 1024
        ),
    )(*in_hbm)


def solution(mesh):
    placed = (P("ctx", "fsdp"), P("fsdp", None), P("ctx", "fsdp"), P("fsdp"))
    body = functools.partial(on_device, mesh.shape["ctx"], mesh.shape["fsdp"])
    return jax.shard_map(body, mesh=mesh, in_specs=placed, out_specs=P("ctx", "fsdp"), check_vma=False)
```
